256 devices in a mesh: dom: 64 (over z, y, core), chan: 4 (over x).
Axes of the slice: x: 4, y: 4, z: 8, core: 2. Of those that a mesh axis runs over, the one named last changes fastest.
Arguments:
- features: bfloat16 [256, 65536], P('chan', 'dom'), may hold values from -6 to 6
- cotangent: bfloat16 [256, 65536], P('chan', 'dom'), may hold values from -6 to 6
- weights: bfloat16 [9, 256, 256], P(None, 'chan'), may hold values from -0.375 to 0.375
- tile_values: float32 [4096, 128, 128], P('dom'), may hold values from -0.046875 to 0.046875
- tile_cols: int32 [64, 8, 8], P('dom'), may hold values from 0 to 11, as said below
- send_list: int32 [64, 4, 128], P('dom'), may hold values from 0 to 1023
Outputs:
- input_grad: float32 [256, 65536], P('chan', 'dom')
- weight_grad: float32 [9, 256, 256], P(None, None, 'chan')
The draws below stay inside these ranges and needn't reach their ends.
Inputs may be any that keep to these rules, and one draw needn't show every extreme that they name: `tile_cols`: values below 8 are blocks of the partition's own nodes; 8 + s is the block received from neighbour slot s. Tile 0 of row block r has column block r.
All inputs are finite; a program needn't handle non-finite values.
Results may differ from the reference program's by a relative error of at most 0.0003.
Values may be sent and summed in bfloat16 or wider, within the bound.
A program may use at most 128 MiB of HBM per device.

```python
import jax
import jax.numpy as jnp
from jax import lax

C = 256
TILE = 128
ORDER = 8
TPR = 8
NB_DEV = 8
PARTITIONS = 64
NODES = 65536
TILES = 4096


def draw_tile_cols(key, part):
    columns = jax.random.randint(key, (PARTITIONS, NB_DEV, TPR), 0, NB_DEV).astype(jnp.int32)
    row_ids = jnp.arange(NB_DEV, dtype=jnp.int32)[None, :]
    columns = columns.at[:, :, 0].set(row_ids)
    columns = columns.at[:, :, TPR - 2].set(NB_DEV + row_ids % 4)
    columns = columns.at[:, :, TPR - 1].set(NB_DEV + (row_ids + 2) % 4)
    return columns.astype(jnp.int32)


def set_ends(array, key, smallest, high):
    index_at = [jax.random.randint(jax.random.fold_in(key, axis), (), 0, length) for axis, length in enumerate(array.shape)]
    longest = array.shape.index(max(array.shape))
    beside = index_at[:longest] + [(index_at[longest] + 1) % array.shape[longest]] + index_at[longest + 1:]
    return array.at[tuple(index_at)].set(smallest).at[tuple(beside)].set(high)


def level_of(stream_key, extent, split, low, top_value):
    level, own = 1.0, jax.random.fold_in(stream_key, 6)
    for position, blocks in split:
        steps = jnp.exp(jax.random.uniform(jax.random.fold_in(own, position), (blocks,), jnp.float32, low / len(split), top_value / len(split)))
        level = level * jnp.repeat(steps, extent[position] // blocks).reshape([-1 if axis == position else 1 for axis in range(len(extent))])
    return level


def bell_draw(rng, shape, scale, bound, pieces=(), held_as=jnp.bfloat16):
    values = scale * jax.random.normal(rng, shape, jnp.float32)
    if pieces:
        values = values * level_of(rng, shape, pieces, -0.22, 0.18)
    return jnp.clip(values, -bound, bound).astype(held_as)


def setup_inputs(seed: int = 0) -> dict:
    key_list = jax.random.split(jax.random.key(seed), 7)
    return {
        "features": bell_draw(key_list[0], (C, NODES), 1.0, 6.0, ((0, 4), (1, 64))),
        "cotangent": bell_draw(key_list[1], (C, NODES), 1.0, 6.0, ((0, 4), (1, 64))),
        "weights": bell_draw(key_list[2], (ORDER + 1, C, C), C ** -0.5, 0.375, ((1, 4),)),
        "tile_values": bell_draw(key_list[3], (TILES, TILE, TILE), (16 * TPR * TILE) ** -0.5, 0.046875, ((0, 64),), jnp.float32),
        "tile_cols": draw_tile_cols(jax.random.fold_in(key_list[6], 71), 0),
        "send_list": set_ends(jax.random.randint(key_list[5], (PARTITIONS, 4, TILE), 0, NB_DEV * TILE), jax.random.fold_in(key_list[5], 1), 0, (NB_DEV * TILE) - 1).astype(jnp.int32),
    }


NEIGHBOUR_SHIFTS = (1, -1, 2, -2)


def take_rows(source_part, row_ids):
    return jnp.take(source_part, row_ids, axis=1)


def apply_operator(field_in, tile_values, tile_cols, send_list):
    channels = field_in.shape[0]
    local_nodes = NB_DEV * TILE
    by_part = field_in.reshape(channels, PARTITIONS, local_nodes).transpose(1, 0, 2)
    halos = []
    for slot_index, offset in enumerate(NEIGHBOUR_SHIFTS):
        source = jnp.roll(by_part, offset, axis=0)
        row_ids = jnp.roll(send_list[:, slot_index, :], offset, axis=0).astype(jnp.int32)
        halos.append(jax.vmap(take_rows)(source, row_ids))
    extended = jnp.concatenate([by_part] + halos, axis=2)
    tiles_part = tile_values.reshape(PARTITIONS, NB_DEV * TPR, TILE, TILE)
    cols_part = tile_cols.reshape(PARTITIONS, NB_DEV * TPR).astype(jnp.int32)

    def one_part(operands):
        ext_part, tile_part, col_part = operands
        blocks = ext_part.reshape(channels, NB_DEV + 4, TILE)
        picked = jnp.take(blocks, col_part, axis=1)
        product = jnp.einsum('ctj,tjk->ctk', picked, tile_part, precision=lax.Precision.HIGHEST)
        return product.reshape(channels, NB_DEV, TPR, TILE).sum(axis=2).reshape(channels, local_nodes)

    result = lax.map(one_part, (extended, tiles_part, cols_part))
    return result.transpose(1, 0, 2).reshape(channels, PARTITIONS * local_nodes)


def reference(features, cotangent, weights, tile_values, tile_cols, send_list):
    feat_wide = features.astype(jnp.float32)
    cot_wide = cotangent.astype(jnp.float32)

    def operator_on(field_in):
        return apply_operator(field_in, tile_values, tile_cols, send_list)

    def mixed_term(order_index):
        return jnp.dot(weights[order_index].astype(jnp.float32), cot_wide, precision=lax.Precision.HIGHEST)

    def grad_term(state):
        return lax.dot_general(feat_wide, state, (((1,), (1,)), ((), ())), precision=lax.Precision.HIGHEST)

    cheb_prev = cot_wide
    grad_terms = [grad_term(cheb_prev)]
    cheb_now = operator_on(cheb_prev)
    grad_terms.append(grad_term(cheb_now))
    for order_index in range(2, ORDER + 1):
        cheb_prev, cheb_now = cheb_now, 2.0 * operator_on(cheb_now) - cheb_prev
        grad_terms.append(grad_term(cheb_now))
    current = mixed_term(ORDER)
    clen_later = jnp.zeros_like(current)
    for order_index in range(ORDER - 1, 0, -1):
        current, clen_later = mixed_term(order_index) + 2.0 * operator_on(current) - clen_later, current
    input_grad = mixed_term(0) + operator_on(current) - clen_later
    weight_grad = jnp.stack(grad_terms) * (float(NODES) ** -0.5)
    return input_grad, weight_grad
```

```python
import functools

import jax
import jax.numpy as jnp
from jax import lax
from jax.experimental import pallas as pl
from jax.experimental.pallas import tpu as pltpu
from jax.sharding import PartitionSpec as P

NEIGHBOUR_SHIFTS = (1, -1, 2, -2)
SLOTS = len(NEIGHBOUR_SHIFTS)
MESH = pl.DeviceIdType.MESH
F32, BF16 = jnp.float32, jnp.bfloat16


def dot(a, b):
    return jnp.dot(a, b, preferred_element_type=F32)


def dot_nt(a, b):
    return lax.dot_general(a, b, (((1,), (1,)), ((), ())), preferred_element_type=F32)


def split(x):
    hi = x.astype(BF16)
    return hi, (x - hi.astype(F32)).astype(BF16)


def kernel(
    dims,
    feat_hbm, cot_hbm, w_hbm, tiles_hbm, cols_hbm, send_hbm,
    grad_out, wg_out,
    feat, cotx, w, tiles, cols, send, sel, e_hi, e_lo, state, parts, base,
    outbox, inbox, wg, wg_rows, wg_deep, wg_full,
    local_sem, tile_sem, out_sem, gather_send, gather_recv, halo_send, halo_recv,
    s1, s2, s3, r1, r2, r3,
):
    dom, chan, group, scale = dims
    depth = dom // group
    me, xc = lax.axis_index("dom"), lax.axis_index("chan")
    zc, bc = me // group, lax.rem(me, group)
    top = w.shape[0] - 1
    c, n = feat_hbm.shape
    tile = tiles.shape[-1]
    halo = SLOTS * tile
    blocks = n // tile
    wide = n + halo
    per_row = tiles.shape[0] // blocks
    share = c // group

    def along_dom(index):
        return {"dom": index}

    halo_to = [along_dom(lax.rem(me + d + dom, dom)) for d in NEIGHBOUR_SHIFTS]
    chan_of = [lax.rem(xc + j, chan) for j in range(1, chan)]
    row_of = [lax.rem(bc + j, group) for j in range(1, group)]
    deep_of = [lax.rem(zc + j, depth) for j in range(1, depth)]
    row_to = [along_dom(zc * group + b) for b in row_of]
    deep_to = [along_dom(z * group + bc) for z in deep_of]

    def remote(src, dst, ssem, rsem, to):
        return pltpu.make_async_remote_copy(src, dst, ssem, rsem, device_id=to, device_id_type=MESH)

    my_rows = pl.ds(pl.multiple_of(xc * c, c), c)
    own_cot = cotx.at[my_rows, pl.ds(0, n)]
    own_feat = feat.at[my_rows, :]
    in_copies = [
        pltpu.make_async_copy(send_hbm, send, local_sem.at[0]),
        pltpu.make_async_copy(cot_hbm, own_cot, local_sem.at[1]),
        pltpu.make_async_copy(cols_hbm, cols, local_sem.at[2]),
        pltpu.make_async_copy(w_hbm, w, local_sem.at[3]),
        pltpu.make_async_copy(feat_hbm, own_feat, local_sem.at[4]),
    ]
    for copy in in_copies:
        copy.start()

    def tile_copy(r):
        rows = pl.ds(r * per_row, per_row)
        return pltpu.make_async_copy(tiles_hbm.at[rows], tiles.at[rows], tile_sem.at[r])

    for r in range(blocks):
        tile_copy(r).start()

    barrier = pltpu.get_barrier_semaphore()
    greeted = halo_to + [{"chan": x} for x in chan_of] + row_to + deep_to
    for peer in greeted:
        pl.semaphore_signal(barrier, inc=1, device_id=peer, device_id_type=MESH)

    in_copies[0].wait()
    node = lax.broadcasted_iota(jnp.int32, (n, tile), 0)
    for s in range(SLOTS):
        picked = send[0, s : s + 1, :]
        sel[:, s * tile : (s + 1) * tile] = jnp.where(node == picked, 1.0, 0.0).astype(BF16)
    in_copies[1].wait()
    first = cotx[my_rows, 0:n]
    first_sel = dot(first, sel[...])
    state[0, 0:c, 0:n] = first.astype(F32)
    state[0, 0:c, n:wide] = first_sel
    state[0, c:, :] = jnp.zeros((c, wide), F32)
    state[1] = jnp.zeros((2 * c, wide), F32)
    parts[...] = jnp.zeros(parts.shape, BF16)
    parts[0:c] = first
    for s in range(SLOTS):
        outbox[0, s] = jnp.zeros(outbox.shape[2:], BF16)
        outbox[0, s, 0:c] = first_sel[:, s * tile : (s + 1) * tile].astype(BF16)

    def halo_copy(parity, s):
        return remote(
            outbox.at[parity, s], inbox.at[parity, s], halo_send.at[parity, s], halo_recv.at[parity, s], halo_to[s]
        )

    def gather_copy(which, j):
        src = (cot_hbm, feat_hbm)[which]
        dst = (own_cot, own_feat)[which]
        return remote(src, dst, gather_send.at[which, j], gather_recv.at[which, xc], {"chan": chan_of[j]})

    def gather_wait(which):
        for x in chan_of:
            rows = pl.ds(pl.multiple_of(x * c, c), c)
            dst = (cotx.at[rows, pl.ds(0, n)], feat.at[rows, :])[which]
            src = (cot_hbm, feat_hbm)[which]
            remote(src, dst, gather_send.at[which, 0], gather_recv.at[which, x], {"chan": x}).wait_recv()

    pl.semaphore_wait(barrier, len(greeted))
    for s in range(SLOTS):
        halo_copy(0, s).start()
    for which in range(2):
        for j in range(chan - 1):
            gather_copy(which, j).start()

    in_copies[2].wait()

    def assemble(r, carry):
        tile_copy(r).wait()
        columns = pl.ds(pl.multiple_of(r * tile, tile), tile)
        marks = [cols[0, r, j] for j in range(per_row)]

        def block(cb, carry):
            total = jnp.zeros((tile, tile), F32)
            for j in range(per_row):
                total += jnp.where(marks[j] == cb, 1.0, 0.0) * tiles[r * per_row + j]
            hi, lo = split(total)
            rows = pl.ds(pl.multiple_of(cb * tile, tile), tile)
            e_hi[rows, columns] = hi
            e_lo[rows, columns] = lo
            return carry

        return lax.fori_loop(0, blocks + SLOTS, block, carry)

    lax.fori_loop(0, blocks, assemble, 0)

    def extend(i, carry):
        rows = pl.ds(pl.multiple_of(i * 2 * tile, 2 * tile), 2 * tile)
        e_hi[rows, n:wide] = dot(e_hi[rows, 0:n], sel[...]).astype(BF16)
        e_lo[rows, n:wide] = dot(e_lo[rows, 0:n], sel[...]).astype(BF16)
        return carry

    lax.fori_loop(0, wide // (2 * tile), extend, 0)

    in_copies[3].wait()
    gather_wait(0)
    cotx[:, n:wide] = dot(cotx[:, 0:n], sel[...]).astype(BF16)

    chunk = halo

    def prepare(order, fac_u, fac_b, older):
        for i in range(wide // chunk):
            at = slice(i * chunk, (i + 1) * chunk)
            full = dot(parts[...], e_hi[0:n, at])
            part = full[0 : 2 * c] + full[2 * c :] + dot(parts[0 : 2 * c], e_lo[0:n, at])
            base[0:c, at] = fac_u * part[0:c] - state[older, 0:c, at]
            base[c:, at] = fac_b * part[c:] + dot(w[order], cotx[:, at]) - state[older, c:, at]

    def arrived(lhs, at):
        full = dot(lhs, e_hi[n:wide, at])
        return full[0 : 2 * c] + full[2 * c :] + dot(lhs[0 : 2 * c], e_lo[n:wide, at])

    def halo_in(parity):
        for s in range(SLOTS):
            halo_copy(parity, s).wait_recv()
        return jnp.concatenate([inbox[parity, s] for s in range(SLOTS)], axis=1)

    def row_part(b):
        return pl.ds(pl.multiple_of(b * share, share), share)

    def step1(k, j, sem_of):
        return remote(wg.at[k, row_part(row_of[j])], wg_rows.at[k, sem_of], s1.at[j], r1.at[k, sem_of], row_to[j])

    def step2(k, j, sem_of):
        return remote(wg_deep.at[k, sem_of], wg_deep.at[k, sem_of], s2.at[j], r2.at[k, sem_of], deep_to[j])

    def step3(k, j, sem_of):
        part = wg_full.at[k, row_part(sem_of)]
        return remote(part, part, s3.at[j], r3.at[k, sem_of], row_to[j])

    def send_rows(k, again):
        for j in range(group - 1):
            if again:
                step1(k, j, bc).wait_send()
        wg_rows[k, bc] = wg[k, row_part(bc), :]
        for j in range(group - 1):
            step1(k, j, bc).start()

    def send_deep(k, again):
        for j in range(group - 1):
            step1(k, j, row_of[j]).wait_recv()
        for j in range(depth - 1):
            if again:
                step2(k, j, zc).wait_send()
        total = wg_rows[k, 0]
        for j in range(1, group):
            total += wg_rows[k, j]
        wg_deep[k, zc] = total
        for j in range(depth - 1):
            step2(k, j, zc).start()

    def send_back(k, again):
        for j in range(depth - 1):
            step2(k, j, deep_of[j]).wait_recv()
        for j in range(group - 1):
            if again:
                step3(k, j, bc).wait_send()
        total = wg_deep[k, 0]
        for j in range(1, depth):
            total += wg_deep[k, j]
        wg_full[k, row_part(bc), :] = total * scale
        for j in range(group - 1):
            step3(k, j, bc).start()

    prepare(top, 1.0, 2.0, 1)

    def round_(r, carry):
        parity = lax.rem(r, 2)
        other = 1 - parity
        fac_u = jnp.where(r == 0, 1.0, 2.0).astype(F32)
        lhs = halo_in(parity)
        at = slice(n, wide)
        got = arrived(lhs, at)
        next_u = base[0:c, at] + fac_u * got[0:c]
        next_b = base[c:, at] + 2.0 * got[c:]
        state[other, 0:c, at] = next_u
        state[other, c:, at] = next_b
        u_hi, u_lo = split(next_u)
        b_hi, b_lo = split(next_b)

        @pl.when(r > 0)
        def _():
            for s in range(SLOTS):
                halo_copy(other, s).wait_send()

        for s in range(SLOTS):
            cut = slice(s * tile, (s + 1) * tile)
            for i, piece in enumerate((u_hi, b_hi, u_lo, b_lo)):
                outbox[other, s, i * c : (i + 1) * c] = piece[:, cut]
        for s in range(SLOTS):
            halo_copy(other, s).start()
        for i in range(n // chunk):
            at = slice(i * chunk, (i + 1) * chunk)
            got = arrived(lhs, at)
            next_u = base[0:c, at] + fac_u * got[0:c]
            next_b = base[c:, at] + 2.0 * got[c:]
            state[other, 0:c, at] = next_u
            state[other, c:, at] = next_b
            for j, piece in enumerate((*split(next_u), *split(next_b))):
                row = (0, 2, 1, 3)[j] * c
                parts[row : row + c, at] = piece

        @pl.when(r == 0)
        def _():
            in_copies[4].wait()
            gather_wait(1)
            wg[0] = dot_nt(cotx[my_rows, 0:n], feat[...])
            send_rows(0, False)

        both = dot_nt(jnp.concatenate([parts[0:c], parts[2 * c : 3 * c]], axis=0), feat[...])
        wg[r + 1] = both[0:c] + both[c:]
        prepare(top - 1 - r, 2.0, jnp.where(r == top - 1, 1.0, 2.0).astype(F32), parity)

        @pl.when(r == 2)
        def _():
            send_back(0, False)

        @pl.when(r >= 2)
        def _():
            send_back(r - 1, True)

        @pl.when(r == 1)
        def _():
            send_deep(0, False)

        @pl.when(r >= 1)
        def _():
            send_deep(r, True)

        send_rows(r + 1, True)
        return carry

    lax.fori_loop(0, top, round_, 0)

    send_deep(top, True)
    last = top % 2
    lhs = halo_in(last)
    for i in range(n // chunk):
        at = slice(i * chunk, (i + 1) * chunk)
        base[c:, at] = base[c:, at] + arrived(lhs, at)[c:]
    grad_copy = pltpu.make_async_copy(base.at[pl.ds(c, c), pl.ds(0, n)], grad_out, out_sem.at[0])
    grad_copy.start()
    send_back(top - 1, True)
    for k in range(top):
        for j in range(group - 1):
            step3(k, j, row_of[j]).wait_recv()
    early = pltpu.make_async_copy(wg_full.at[pl.ds(0, top)], wg_out.at[pl.ds(0, top)], out_sem.at[1])
    early.start()
    send_back(top, True)
    for j in range(group - 1):
        step3(top, j, row_of[j]).wait_recv()
    late = pltpu.make_async_copy(wg_full.at[top], wg_out.at[top], out_sem.at[2])
    late.start()

    for which in range(2):
        for j in range(chan - 1):
            gather_copy(which, j).wait_send()
    for parity in range(2):
        for s in range(SLOTS):
            halo_copy(parity, s).wait_send()
    for j in range(group - 1):
        step1(top, j, bc).wait_send()
        step3(top, j, bc).wait_send()
    for j in range(depth - 1):
        step2(top, j, zc).wait_send()
    grad_copy.wait()
    early.wait()
    late.wait()


def local(dom, chan, group, features, cotangent, weights, tile_values, tile_cols, send_list):
    c, n = features.shape
    orders, _, all_c = weights.shape
    tiles, tile, _ = tile_values.shape
    halo = SLOTS * tile
    wide = n + halo
    depth, share = dom // group, c // group
    scale = float(dom * n) ** -0.5
    dma, vmem = pltpu.SemaphoreType.DMA, pltpu.VMEM
    anywhere = pl.BlockSpec(memory_space=pl.ANY)
    input_grad, weight_grad = pl.pallas_call(
        functools.partial(kernel, (dom, chan, group, scale)),
        out_shape=(
            jax.ShapeDtypeStruct((c, n), F32),
            jax.ShapeDtypeStruct((orders, c, all_c), F32),
        ),
        in_specs=[anywhere] * 6,
        out_specs=(anywhere, anywhere),
        scratch_shapes=[
            vmem((all_c, n), BF16),
            vmem((all_c, wide), BF16),
            vmem(weights.shape, BF16),
            vmem(tile_values.shape, F32),
            pltpu.SMEM(tile_cols.shape, jnp.int32),
            vmem(send_list.shape, jnp.int32),
            vmem((n, halo), BF16),
            vmem((wide, wide), BF16),
            vmem((wide, wide), BF16),
            vmem((2, 2 * c, wide), F32),
            vmem((4 * c, n), BF16),
            vmem((2 * c, wide), F32),
            vmem((2, SLOTS, 4 * c, tile), BF16),
            vmem((2, SLOTS, 4 * c, tile), BF16),
            vmem((orders, c, all_c), F32),
            vmem((orders, group, share, all_c), F32),
            vmem((orders, depth, share, all_c), F32),
            vmem((orders, c, all_c), F32),
            dma((5,)),
            dma((n // tile,)),
            dma((3,)),
            dma((2, chan)),
            dma((2, chan)),
            dma((2, SLOTS)),
            dma((2, SLOTS)),
            dma((group,)),
            dma((depth,)),
            dma((group,)),
            dma((orders, group)),
            dma((orders, depth)),
            dma((orders, group)),
        ],
        compiler_params=pltpu.CompilerParams(
            collective_id=0, has_side_effects=True, vmem_limit_bytes=48 << 20
        ),
        name="clenshaw",
    )(features, cotangent, weights, tile_values, tile_cols, send_list)
    return input_grad, jnp.swapaxes(weight_grad, 1, 2)


def solution(mesh):
    dom, chan = mesh.shape["dom"], mesh.shape["chan"]
    placed = (
        P("chan", "dom"),
        P("chan", "dom"),
        P(None, "chan", None),
        P("dom", None, None),
        P("dom", None, None),
        P("dom", None, None),
    )
    return jax.shard_map(
        functools.partial(local, dom, chan, 8),
        mesh=mesh,
        in_specs=placed,
        out_specs=(P("chan", "dom"), P(None, None, "chan")),
        check_vma=False,
    )
```

```python
import functools

import jax
import jax.numpy as jnp
from jax import lax
from jax.experimental import pallas as pl
from jax.experimental.pallas import tpu as pltpu
from jax.sharding import PartitionSpec as P

NEIGHBOUR_SHIFTS = (1, -1, 2, -2)
SLOTS = len(NEIGHBOUR_SHIFTS)
MESH = pl.DeviceIdType.MESH
BATCHES = ((0, 3), (3, 6), (6, 7), (7, 8), (8, 9))
F32, BF16 = jnp.float32, jnp.bfloat16


def dot(a, b):
    return jnp.dot(a, b, preferred_element_type=F32)


def dot_nt(a, b):
    return lax.dot_general(a, b, (((1,), (1,)), ((), ())), preferred_element_type=F32)


def split(x):
    hi = x.astype(BF16)
    return hi, (x - hi.astype(F32)).astype(BF16)


def kernel(
    dims,
    feat_hbm, cot_hbm, w_hbm, tiles_hbm, cols_hbm, send_hbm,
    grad_out, wg_out,
    feat, cotx, w, tiles, sums, cols, send, sel, e_hi, e_lo, state, parts, base,
    outbox, inbox, early, wg, wg_rows, wg_deep, wg_full,
    local_sem, tile_sem, out_sem, gather_send, gather_recv, halo_send, halo_recv,
    s1, s2, s3, r1, r2, r3,
):
    dom, chan, group, scale = dims
    depth = dom // group
    me, xc = lax.axis_index("dom"), lax.axis_index("chan")
    zc, bc = me // group, lax.rem(me, group)
    top = w.shape[0] - 1
    c, n = feat_hbm.shape
    tile = tiles.shape[-1]
    halo = SLOTS * tile
    blocks = n // tile
    wide = n + halo
    per_row = tiles.shape[0] // blocks
    share = c // group

    def along_dom(index):
        return {"dom": index}

    halo_to = [along_dom(lax.rem(me + d + dom, dom)) for d in NEIGHBOUR_SHIFTS]
    chan_of = [lax.rem(xc + j, chan) for j in range(1, chan)]
    row_of = [lax.rem(bc + j, group) for j in range(1, group)]
    deep_of = [lax.rem(zc + j, depth) for j in range(1, depth)]
    row_to = [along_dom(zc * group + b) for b in row_of]
    deep_to = [along_dom(z * group + bc) for z in deep_of]

    def remote(src, dst, ssem, rsem, to):
        return pltpu.make_async_remote_copy(src, dst, ssem, rsem, device_id=to, device_id_type=MESH)

    my_rows = pl.ds(pl.multiple_of(xc * c, c), c)
    own_cot = cotx.at[my_rows, pl.ds(0, n)]
    own_feat = feat.at[my_rows, :]
    in_copies = [
        pltpu.make_async_copy(send_hbm, send, local_sem.at[0]),
        pltpu.make_async_copy(cot_hbm, own_cot, local_sem.at[1]),
        pltpu.make_async_copy(cols_hbm, cols, local_sem.at[2]),
        pltpu.make_async_copy(w_hbm, w, local_sem.at[3]),
        pltpu.make_async_copy(feat_hbm, own_feat, local_sem.at[4]),
    ]
    for copy in in_copies:
        copy.start()

    def tile_copy(r):
        rows = pl.ds(r * per_row, per_row)
        return pltpu.make_async_copy(tiles_hbm.at[rows], tiles.at[rows], tile_sem.at[r])

    for r in range(blocks):
        tile_copy(r).start()

    barrier = pltpu.get_barrier_semaphore()
    greeted = halo_to + [{"chan": x} for x in chan_of] + row_to + deep_to
    for peer in greeted:
        pl.semaphore_signal(barrier, inc=1, device_id=peer, device_id_type=MESH)

    in_copies[0].wait()
    node = lax.broadcasted_iota(jnp.int32, (n, tile), 0)
    for s in range(SLOTS):
        picked = send[0, s : s + 1, :]
        sel[:, s * tile : (s + 1) * tile] = jnp.where(node == picked, 1.0, 0.0).astype(BF16)
    in_copies[1].wait()
    first = cotx[my_rows, 0:n]
    first_sel = dot(first, sel[...])
    state[0, 0:c, 0:n] = first.astype(F32)
    state[0, 0:c, n:wide] = first_sel
    cotx[my_rows, n:wide] = first_sel.astype(BF16)
    state[0, c:, :] = jnp.zeros((c, wide), F32)
    state[1] = jnp.zeros((2 * c, wide), F32)
    parts[...] = jnp.zeros(parts.shape, BF16)
    parts[0:c] = first
    for s in range(SLOTS):
        outbox[0, s] = jnp.zeros(outbox.shape[2:], BF16)
        outbox[0, s, 0:c] = first_sel[:, s * tile : (s + 1) * tile].astype(BF16)

    def halo_copy(parity, s):
        return remote(
            outbox.at[parity, s], inbox.at[parity, s], halo_send.at[parity, s], halo_recv.at[parity, s], halo_to[s]
        )

    def gathered(which, x):
        rows = pl.ds(pl.multiple_of(x * c, c), c)
        return (cotx.at[rows, pl.ds(n, halo)], cotx.at[rows, pl.ds(0, n)], feat.at[rows, :])[which]

    def gather_copy(which, j):
        block = gathered(which, xc)
        return remote(block, block, gather_send.at[which, j], gather_recv.at[which, xc], {"chan": chan_of[j]})

    def gather_wait(which):
        for x in chan_of:
            block = gathered(which, x)
            remote(block, block, gather_send.at[which, 0], gather_recv.at[which, x], {"chan": x}).wait_recv()

    pl.semaphore_wait(barrier, len(greeted))
    for s in range(SLOTS):
        halo_copy(0, s).start()
    for which in range(2):
        for j in range(chan - 1):
            gather_copy(which, j).start()

    in_copies[2].wait()

    sums[per_row] = jnp.zeros((tile, tile), F32)

    def assemble(r, carry):
        tile_copy(r).wait()
        columns = pl.ds(pl.multiple_of(r * tile, tile), tile)
        block_of = [cols[0, r, j] for j in range(per_row)]
        for j in range(per_row):
            before = per_row
            for i in range(j):
                before = jnp.where(block_of[i] == block_of[j], i, before)
            mine = tiles[r * per_row + j]
            sums[j] = mine if j == 0 else mine + sums[before]
        for cb in range(blocks + SLOTS):
            last = per_row
            for j in range(per_row):
                last = jnp.where(block_of[j] == cb, j, last)
            hi, lo = split(sums[last])
            e_hi[cb * tile : (cb + 1) * tile, columns] = hi
            e_lo[cb * tile : (cb + 1) * tile, columns] = lo
        return carry

    lax.fori_loop(0, blocks, assemble, 0)

    for e in (e_hi, e_lo):
        for i in range(SLOTS // 2):
            at = slice(2 * i * tile, 2 * (i + 1) * tile)
            e[:, n + 2 * i * tile : n + 2 * (i + 1) * tile] = dot(e[:, 0:n], sel[:, at]).astype(BF16)

    chunk = halo

    def prepare(order, fac_u, fac_b, older):
        for i in range(wide // chunk):
            at = slice(i * chunk, (i + 1) * chunk)
            full = dot(parts[...], e_hi[0:n, at])
            part = full[0 : 2 * c] + full[2 * c :] + dot(parts[0 : 2 * c], e_lo[0:n, at])
            base[0:c, at] = fac_u * part[0:c] - state[older, 0:c, at]
            base[c:, at] = fac_b * part[c:] - state[older, c:, at]
            if order is not None:
                base[c:, at] += dot(w[order], cotx[:, at])

    def arrived(lhs, at):
        full = dot(lhs, e_hi[n:wide, at])
        return full[0 : 2 * c] + full[2 * c :] + dot(lhs[0 : 2 * c], e_lo[n:wide, at])

    def halo_in(parity):
        for s in range(SLOTS):
            halo_copy(parity, s).wait_recv()
        return jnp.concatenate([inbox[parity, s] for s in range(SLOTS)], axis=1)

    def row_part(b):
        return pl.ds(pl.multiple_of(b * share, share), share)

    def orders_of(i):
        low, high = BATCHES[i]
        return pl.ds(low, high - low)

    def step1(i, j, sem_of):
        k = orders_of(i)
        return remote(wg.at[k, row_part(row_of[j])], wg_rows.at[sem_of, k], s1.at[i, j], r1.at[i, sem_of], row_to[j])

    def step2(i, j, sem_of):
        part = wg_deep.at[sem_of, orders_of(i)]
        return remote(part, part, s2.at[i, j], r2.at[i, sem_of], deep_to[j])

    def step3(i, j, sem_of):
        part = wg_full.at[orders_of(i), row_part(sem_of)]
        return remote(part, part, s3.at[i, j], r3.at[i, sem_of], row_to[j])

    def send_rows(i):
        k = orders_of(i)
        for j in range(group - 1):
            step1(i, j, bc).start()
        wg_rows[bc, k] = wg[k, row_part(bc), :]

    def send_deep(i):
        k = orders_of(i)
        for j in range(group - 1):
            step1(i, j, row_of[j]).wait_recv()
        total = wg_rows[0, k]
        for j in range(1, group):
            total += wg_rows[j, k]
        wg_deep[zc, k] = total
        for j in range(depth - 1):
            step2(i, j, zc).start()

    def send_back(i):
        k = orders_of(i)
        for j in range(depth - 1):
            step2(i, j, deep_of[j]).wait_recv()
        total = wg_deep[0, k]
        for j in range(1, depth):
            total += wg_deep[j, k]
        wg_full[k, row_part(bc), :] = total * scale
        for j in range(group - 1):
            step3(i, j, bc).start()

    def at_round(r, when, step, among=range(len(BATCHES))):
        for i in among:
            if when(BATCHES[i][1]) < top:
                pl.when(r == when(BATCHES[i][1]))(functools.partial(step, i))

    def deep_round(high):
        return high - 1

    def back_round(high):
        return high + 1 if high < top - 1 else high

    prepare(None, 1.0, 2.0, 1)
    in_copies[3].wait()
    gather_wait(0)
    base[c:, n:wide] += dot(w[top], cotx[:, n:wide])

    def round_(r, carry):
        parity = lax.rem(r, 2)
        other = 1 - parity
        fac_u = jnp.where(r == 0, 1.0, 2.0).astype(F32)
        lhs = halo_in(parity)
        at = slice(n, wide)
        got = arrived(lhs, at)
        next_u = base[0:c, at] + fac_u * got[0:c]
        next_b = base[c:, at] + 2.0 * got[c:]
        state[other, 0:c, at] = next_u
        state[other, c:, at] = next_b
        u_hi, u_lo = split(next_u)
        b_hi, b_lo = split(next_b)

        @pl.when(r > 0)
        def _():
            for s in range(SLOTS):
                halo_copy(other, s).wait_send()

        for s in range(SLOTS):
            cut = slice(s * tile, (s + 1) * tile)
            for i, piece in enumerate((u_hi, b_hi, u_lo, b_lo)):
                outbox[other, s, i * c : (i + 1) * c] = piece[:, cut]
        for s in range(SLOTS):
            halo_copy(other, s).start()

        @pl.when(r == 0)
        def _():
            gather_wait(1)
            in_copies[4].wait()
            for j in range(chan - 1):
                gather_copy(2, j).start()
            base[c:, 0:n] += dot(w[top], cotx[:, 0:n])

        for i in range(n // chunk):
            at = slice(i * chunk, (i + 1) * chunk)
            got = arrived(lhs, at)
            next_u = base[0:c, at] + fac_u * got[0:c]
            next_b = base[c:, at] + 2.0 * got[c:]
            state[other, 0:c, at] = next_u
            state[other, c:, at] = next_b
            for j, piece in enumerate((*split(next_u), *split(next_b))):
                row = (0, 2, 1, 3)[j] * c
                parts[row : row + c, at] = piece

        def now():
            return jnp.concatenate([parts[0:c], parts[2 * c : 3 * c]], axis=0)

        def weigh(k, field):
            both = dot_nt(field, feat[...])
            wg[k] = both[0:c] + both[c:]

        @pl.when(r == 0)
        def _():
            early[...] = now()

        @pl.when(r > 1)
        def _():
            weigh(r + 1, now())

        at_round(r, lambda high: high - 2, send_rows, range(1, len(BATCHES)))
        prepare(top - 1 - r, 2.0, jnp.where(r == top - 1, 1.0, 2.0).astype(F32), parity)

        @pl.when(r == 1)
        def _():
            gather_wait(2)
            wg[0] = dot_nt(cotx[my_rows, 0:n], feat[...])
            weigh(1, early[...])
            weigh(2, now())
            send_rows(0)

        at_round(r, back_round, send_back)
        at_round(r, deep_round, send_deep)
        return carry

    lax.fori_loop(0, top, round_, 0)

    for i, (_, high) in enumerate(BATCHES):
        if deep_round(high) >= top:
            send_deep(i)
    last = top % 2
    lhs = halo_in(last)
    for i in range(n // chunk):
        at = slice(i * chunk, (i + 1) * chunk)
        base[c:, at] = base[c:, at] + arrived(lhs, at)[c:]
    grad_copy = pltpu.make_async_copy(base.at[pl.ds(c, c), pl.ds(0, n)], grad_out, out_sem.at[0])
    grad_copy.start()
    for i, (_, high) in enumerate(BATCHES):
        if back_round(high) >= top:
            send_back(i)
    for i in range(len(BATCHES)):
        for j in range(group - 1):
            step3(i, j, row_of[j]).wait_recv()
    wg_copy = pltpu.make_async_copy(wg_full, wg_out, out_sem.at[1])
    wg_copy.start()

    for which in range(3):
        for j in range(chan - 1):
            gather_copy(which, j).wait_send()
    for parity in range(2):
        for s in range(SLOTS):
            halo_copy(parity, s).wait_send()
    for i in range(len(BATCHES)):
        for j in range(group - 1):
            step1(i, j, bc).wait_send()
            step3(i, j, bc).wait_send()
        for j in range(depth - 1):
            step2(i, j, zc).wait_send()
    grad_copy.wait()
    wg_copy.wait()


def local(dom, chan, group, *arrays):
    features, _, weights, tile_values, tile_cols, send_list = arrays
    c, n = features.shape
    orders, _, all_c = weights.shape
    tiles, tile, _ = tile_values.shape
    halo = SLOTS * tile
    wide = n + halo
    depth, share = dom // group, c // group
    scale = float(dom * n) ** -0.5
    dma, vmem = pltpu.SemaphoreType.DMA, pltpu.VMEM
    anywhere = pl.BlockSpec(memory_space=pl.ANY)
    input_grad, weight_grad = pl.pallas_call(
        functools.partial(kernel, (dom, chan, group, scale)),
        out_shape=(
            jax.ShapeDtypeStruct((c, n), F32),
            jax.ShapeDtypeStruct((orders, c, all_c), F32),
        ),
        in_specs=[anywhere] * 6,
        out_specs=(anywhere, anywhere),
        scratch_shapes=[
            vmem((all_c, n), BF16),
            vmem((all_c, wide), BF16),
            vmem(weights.shape, BF16),
            vmem(tile_values.shape, F32),
            vmem((tile_cols.shape[-1] + 1, tile, tile), F32),
            pltpu.SMEM(tile_cols.shape, jnp.int32),
            vmem(send_list.shape, jnp.int32),
            vmem((n, halo), BF16),
            vmem((wide, wide), BF16),
            vmem((wide, wide), BF16),
            vmem((2, 2 * c, wide), F32),
            vmem((4 * c, n), BF16),
            vmem((2 * c, wide), F32),
            vmem((2, SLOTS, 4 * c, tile), BF16),
            vmem((2, SLOTS, 4 * c, tile), BF16),
            vmem((2 * c, n), BF16),
            vmem((orders, c, all_c), F32),
            vmem((group, orders, share, all_c), F32),
            vmem((depth, orders, share, all_c), F32),
            vmem((orders, c, all_c), F32),
            dma((5,)),
            dma((n // tile,)),
            dma((2,)),
            dma((3, chan)),
            dma((3, chan)),
            dma((2, SLOTS)),
            dma((2, SLOTS)),
            *[dma((len(BATCHES), k)) for k in (group, depth, group)],
            *[dma((len(BATCHES), k)) for k in (group, depth, group)],
        ],
        compiler_params=pltpu.CompilerParams(
            collective_id=0, has_side_effects=True, vmem_limit_bytes=48 << 20
        ),
        name="clenshaw",
    )(*(pltpu.with_memory_space_constraint(x, pltpu.HBM) for x in arrays))
    return input_grad, jnp.swapaxes(weight_grad, 1, 2)


def solution(mesh):
    dom, chan = mesh.shape["dom"], mesh.shape["chan"]
    placed = (
        P("chan", "dom"),
        P("chan", "dom"),
        P(None, "chan", None),
        P("dom", None, None),
        P("dom", None, None),
        P("dom", None, None),
    )
    return jax.shard_map(
        functools.partial(local, dom, chan, 8),
        mesh=mesh,
        in_specs=placed,
        out_specs=(P("chan", "dom"), P(None, None, "chan")),
        check_vma=False,
    )
```

```python
import functools

import jax
import jax.numpy as jnp
from jax import lax
from jax.experimental import pallas as pl
from jax.experimental.pallas import tpu as pltpu
from jax.sharding import PartitionSpec as P

NEIGHBOUR_SHIFTS = (1, -1, 2, -2)
SLOTS = len(NEIGHBOUR_SHIFTS)
MESH = pl.DeviceIdType.MESH
LAST, AFTER = 8, 9
BATCHES = ((0, 3, 1, 3, 5), (3, 5, 3, 4, 6), (5, 7, 5, 6, LAST), (7, 9, 6, 7, AFTER))
ADJOINT = (2, 3, 3, 4)
F32, BF16 = jnp.float32, jnp.bfloat16


def dot(a, b):
    return jnp.dot(a, b, preferred_element_type=F32)


def dot_nt(a, b):
    return lax.dot_general(a, b, (((1,), (1,)), ((), ())), preferred_element_type=F32)


def split(x):
    hi = x.astype(BF16)
    return hi, (x - hi.astype(F32)).astype(BF16)


def kernel(
    dims,
    feat_hbm, cot_hbm, w_hbm, tiles_hbm, cols_hbm, send_hbm,
    grad_out, wg_out,
    feat, cotx, w, tiles, sums, cols, send, sel, e_hi, e_lo, state, parts, base,
    outbox, inbox, early, f_out, f_in, f_own, f_hi, f_lo, wg, wg_rows, wg_deep, wg_full,
    local_sem, tile_sem, out_sem, gather_send, gather_recv, halo_send, halo_recv, f_send, f_recv,
    s1, s2, s3, r1, r2, r3,
):
    dom, chan, group, scale = dims
    depth = dom // group
    me, xc = lax.axis_index("dom"), lax.axis_index("chan")
    zc, bc = me // group, lax.rem(me, group)
    top = w.shape[0] - 1
    c, n = feat_hbm.shape
    tile = tiles.shape[-1]
    halo = SLOTS * tile
    blocks = n // tile
    wide = n + halo
    per_row = tiles.shape[0] // blocks
    share = c // group
    all_c = feat.shape[0]

    def along_dom(index):
        return {"dom": index}

    halo_to = [along_dom(lax.rem(me + d + dom, dom)) for d in NEIGHBOUR_SHIFTS]
    chan_of = [lax.rem(xc + j, chan) for j in range(1, chan)]
    row_of = [lax.rem(bc + j, group) for j in range(1, group)]
    deep_of = [lax.rem(zc + j, depth) for j in range(1, depth)]
    row_to = [along_dom(zc * group + b) for b in row_of]
    deep_to = [along_dom(z * group + bc) for z in deep_of]

    def remote(src, dst, ssem, rsem, to):
        return pltpu.make_async_remote_copy(src, dst, ssem, rsem, device_id=to, device_id_type=MESH)

    my_rows = pl.ds(pl.multiple_of(xc * c, c), c)
    own_cot = cotx.at[my_rows, pl.ds(0, n)]
    own_feat = feat.at[my_rows, :]
    in_copies = [
        pltpu.make_async_copy(send_hbm, send, local_sem.at[0]),
        pltpu.make_async_copy(cot_hbm, own_cot, local_sem.at[1]),
        pltpu.make_async_copy(cols_hbm, cols, local_sem.at[2]),
        pltpu.make_async_copy(w_hbm, w, local_sem.at[3]),
        pltpu.make_async_copy(feat_hbm, own_feat, local_sem.at[4]),
    ]
    for copy in in_copies:
        copy.start()

    def tile_copy(r):
        rows = pl.ds(r * per_row, per_row)
        return pltpu.make_async_copy(tiles_hbm.at[rows], tiles.at[rows], tile_sem.at[r])

    for r in range(blocks):
        tile_copy(r).start()

    barrier = pltpu.get_barrier_semaphore()
    greeted = halo_to + [{"chan": x} for x in chan_of] + row_to + deep_to
    for peer in greeted:
        pl.semaphore_signal(barrier, inc=1, device_id=peer, device_id_type=MESH)

    in_copies[0].wait()
    node = lax.broadcasted_iota(jnp.int32, (n, tile), 0)
    for s in range(SLOTS):
        picked = send[0, s : s + 1, :]
        sel[:, s * tile : (s + 1) * tile] = jnp.where(node == picked, 1.0, 0.0).astype(BF16)
    in_copies[1].wait()
    first = cotx[my_rows, 0:n]
    first_sel = dot(first, sel[...])
    state[0, 0:c, 0:n] = first.astype(F32)
    state[0, 0:c, n:wide] = first_sel
    cotx[my_rows, n:wide] = first_sel.astype(BF16)
    state[0, c:, :] = jnp.zeros((c, wide), F32)
    state[1] = jnp.zeros((2 * c, wide), F32)
    parts[...] = jnp.zeros(parts.shape, BF16)
    parts[0:c] = first
    for s in range(SLOTS):
        outbox[0, s] = jnp.zeros(outbox.shape[2:], BF16)
        outbox[0, s, 0:c] = first_sel[:, s * tile : (s + 1) * tile].astype(BF16)

    def halo_copy(parity, s):
        return remote(
            outbox.at[parity, s], inbox.at[parity, s], halo_send.at[parity, s], halo_recv.at[parity, s], halo_to[s]
        )

    def gathered(which, x):
        rows = pl.ds(pl.multiple_of(x * c, c), c)
        return (cotx.at[rows, pl.ds(n, halo)], cotx.at[rows, pl.ds(0, n)], feat.at[rows, :])[which]

    def gather_copy(which, j):
        block = gathered(which, xc)
        return remote(block, block, gather_send.at[which, j], gather_recv.at[which, xc], {"chan": chan_of[j]})

    def gather_wait(which):
        for x in chan_of:
            block = gathered(which, x)
            remote(block, block, gather_send.at[which, 0], gather_recv.at[which, x], {"chan": x}).wait_recv()

    in_copies[2].wait()

    sums[per_row] = jnp.zeros((tile, tile), F32)

    def assemble(r, carry):
        tile_copy(r).wait()
        columns = pl.ds(pl.multiple_of(r * tile, tile), tile)
        block_of = [cols[0, r, j] for j in range(per_row)]
        for j in range(per_row):
            before = per_row
            for i in range(j):
                before = jnp.where(block_of[i] == block_of[j], i, before)
            mine = tiles[r * per_row + j]
            sums[j] = mine if j == 0 else mine + sums[before]
        for cb in range(blocks + SLOTS):
            last = per_row
            for j in range(per_row):
                last = jnp.where(block_of[j] == cb, j, last)
            hi, lo = split(sums[last])
            e_hi[cb * tile : (cb + 1) * tile, columns] = hi
            e_lo[cb * tile : (cb + 1) * tile, columns] = lo
        return carry

    lax.fori_loop(0, blocks, assemble, 0)

    pl.semaphore_wait(barrier, len(greeted))
    for s in range(SLOTS):
        halo_copy(0, s).start()
    for which in range(2):
        for j in range(chan - 1):
            gather_copy(which, j).start()

    for e in (e_hi, e_lo):
        for i in range(SLOTS // 2):
            at = slice(2 * i * tile, 2 * (i + 1) * tile)
            e[:, n + 2 * i * tile : n + 2 * (i + 1) * tile] = dot(e[:, 0:n], sel[:, at]).astype(BF16)

    chunk = halo

    def prepare(order, fac_u, fac_b, older):
        for i in range(wide // chunk):
            at = slice(i * chunk, (i + 1) * chunk)
            full = dot(parts[...], e_hi[0:n, at])
            part = full[0 : 2 * c] + full[2 * c :] + dot(parts[0 : 2 * c], e_lo[0:n, at])
            base[0:c, at] = fac_u * part[0:c] - state[older, 0:c, at]
            base[c:, at] = fac_b * part[c:] - state[older, c:, at]
            if order is not None:
                base[c:, at] += dot(w[order], cotx[:, at])

    def arrived(lhs, at):
        full = dot(lhs, e_hi[n:wide, at])
        return full[0 : 2 * c] + full[2 * c :] + dot(lhs[0 : 2 * c], e_lo[n:wide, at])

    def halo_in(parity):
        for s in range(SLOTS):
            halo_copy(parity, s).wait_recv()
        return jnp.concatenate([inbox[parity, s] for s in range(SLOTS)], axis=1)

    def row_part(b):
        return pl.ds(pl.multiple_of(b * share, share), share)

    def orders_of(i):
        low, high = BATCHES[i][:2]
        return pl.ds(low, high - low)

    def step1(i, j, sem_of):
        k = orders_of(i)
        return remote(wg.at[k, row_part(row_of[j])], wg_rows.at[sem_of, k], s1.at[i, j], r1.at[i, sem_of], row_to[j])

    def step2(i, j, sem_of):
        part = wg_deep.at[sem_of, orders_of(i)]
        return remote(part, part, s2.at[i, j], r2.at[i, sem_of], deep_to[j])

    def step3(i, j, sem_of):
        part = wg_full.at[orders_of(i), row_part(sem_of)]
        return remote(part, part, s3.at[i, j], r3.at[i, sem_of], row_to[j])

    def send_rows(i):
        k = orders_of(i)
        for j in range(group - 1):
            step1(i, j, bc).start()
        wg_rows[bc, k] = wg[k, row_part(bc), :]

    def send_deep(i):
        k = orders_of(i)
        for j in range(group - 1):
            step1(i, j, row_of[j]).wait_recv()
        total = wg_rows[0, k]
        for j in range(1, group):
            total += wg_rows[j, k]
        wg_deep[zc, k] = total
        for j in range(depth - 1):
            step2(i, j, zc).start()

    def send_back(i):
        k = orders_of(i)
        for j in range(depth - 1):
            step2(i, j, deep_of[j]).wait_recv()
        total = wg_deep[0, k]
        for j in range(1, depth):
            total += wg_deep[j, k]
        wg_full[k, row_part(bc), :] = total * scale
        for j in range(group - 1):
            step3(i, j, bc).start()

    def at_round(r, column, step, among=range(len(BATCHES))):
        for i in among:
            if BATCHES[i][column] < top:
                pl.when(r == BATCHES[i][column])(functools.partial(step, i))

    def adjoint_copy(s):
        to = along_dom(lax.rem(me - NEIGHBOUR_SHIFTS[s] + dom, dom))
        return remote(f_out.at[s], f_in.at[s], f_send.at[s], f_recv.at[s], to)

    def adjoint_rows(rows):
        return dot_nt(e_hi[rows, 0:n], feat[...]) + dot_nt(e_lo[rows, 0:n], feat[...])

    def adjoint_out():
        hi, lo = split(adjoint_rows(slice(n, wide)))
        for s in range(SLOTS):
            rows = slice(s * tile, (s + 1) * tile)
            f_out[s, :, 0:all_c] = hi[rows]
            f_out[s, :, all_c:] = lo[rows]

    def adjoint_send():
        for s in range(SLOTS):
            adjoint_copy(s).start()

    def adjoint_own():
        f_own[...] = adjoint_rows(slice(0, n))

    def adjoint_in():
        for s in range(SLOTS):
            adjoint_copy(s).wait_recv()
        both = dot(sel[...], f_in[...].reshape(halo, 2 * all_c))
        hi, lo = split(f_own[...] + both[:, 0:all_c] + both[:, all_c:])
        f_hi[...] = hi
        f_lo[...] = lo

    prepare(None, 1.0, 2.0, 1)
    in_copies[3].wait()
    gather_wait(0)
    base[c:, n:wide] += dot(w[top], cotx[:, n:wide])

    def round_(r, carry):
        parity = lax.rem(r, 2)
        other = 1 - parity
        fac_u = jnp.where(r == 0, 1.0, 2.0).astype(F32)
        lhs = halo_in(parity)
        at = slice(n, wide)
        got = arrived(lhs, at)
        next_u = base[0:c, at] + fac_u * got[0:c]
        next_b = base[c:, at] + 2.0 * got[c:]
        state[other, 0:c, at] = next_u
        state[other, c:, at] = next_b
        u_hi, u_lo = split(next_u)
        b_hi, b_lo = split(next_b)

        @pl.when(r > 0)
        def _():
            for s in range(SLOTS):
                halo_copy(other, s).wait_send()

        for s in range(SLOTS):
            cut = slice(s * tile, (s + 1) * tile)
            for i, piece in enumerate((u_hi, b_hi, u_lo, b_lo)):
                outbox[other, s, i * c : (i + 1) * c] = piece[:, cut]
        for s in range(SLOTS):
            halo_copy(other, s).start()

        @pl.when(r == 0)
        def _():
            gather_wait(1)
            in_copies[4].wait()
            for j in range(chan - 1):
                gather_copy(2, j).start()
            base[c:, 0:n] += dot(w[top], cotx[:, 0:n])

        pl.when(r == ADJOINT[1])(adjoint_send)
        at_round(r, 3, send_deep)
        at_round(r, 4, send_back)

        for i in range(n // chunk):
            at = slice(i * chunk, (i + 1) * chunk)
            got = arrived(lhs, at)
            next_u = base[0:c, at] + fac_u * got[0:c]
            next_b = base[c:, at] + 2.0 * got[c:]
            state[other, 0:c, at] = next_u
            state[other, c:, at] = next_b
            for j, piece in enumerate((*split(next_u), *split(next_b))):
                row = (0, 2, 1, 3)[j] * c
                parts[row : row + c, at] = piece

        def now():
            return jnp.concatenate([parts[0:c], parts[2 * c : 3 * c]], axis=0)

        def weigh(k, field):
            both = dot_nt(field, feat[...])
            wg[k] = both[0:c] + both[c:]

        @pl.when(r == 0)
        def _():
            early[...] = now()

        @pl.when(jnp.logical_and(r > 1, r < top - 1))
        def _():
            weigh(r + 1, now())

        @pl.when(r == top - 2)
        def _():
            both = dot(now(), f_hi[...])
            twice = both[0:c] + both[c:] + dot(parts[0:c], f_lo[...])
            wg[top] = 2.0 * twice - wg[top - 2]

        at_round(r, 2, send_rows, range(1, len(BATCHES)))
        prepare(top - 1 - r, 2.0, jnp.where(r == top - 1, 1.0, 2.0).astype(F32), parity)

        @pl.when(r == 1)
        def _():
            gather_wait(2)
            wg[0] = dot_nt(cotx[my_rows, 0:n], feat[...])
            weigh(1, early[...])
            weigh(2, now())
            send_rows(0)

        for at, step in zip(ADJOINT[::2] + ADJOINT[3:], (adjoint_out, adjoint_own, adjoint_in)):
            pl.when(r == at)(step)
        return carry

    lax.fori_loop(0, top, round_, 0)

    def send_back_at(place):
        for i in range(len(BATCHES)):
            if BATCHES[i][4] == place:
                send_back(i)

    send_back_at(LAST)
    last = top % 2
    lhs = halo_in(last)
    for i in range(n // chunk):
        at = slice(i * chunk, (i + 1) * chunk)
        base[c:, at] = base[c:, at] + arrived(lhs, at)[c:]
    grad_copy = pltpu.make_async_copy(base.at[pl.ds(c, c), pl.ds(0, n)], grad_out, out_sem.at[0])
    grad_copy.start()
    send_back_at(AFTER)
    for i in range(len(BATCHES)):
        for j in range(group - 1):
            step3(i, j, row_of[j]).wait_recv()
    wg_copy = pltpu.make_async_copy(wg_full, wg_out, out_sem.at[1])
    wg_copy.start()

    for which in range(3):
        for j in range(chan - 1):
            gather_copy(which, j).wait_send()
    for parity in range(2):
        for s in range(SLOTS):
            halo_copy(parity, s).wait_send()
    for i in range(len(BATCHES)):
        for j in range(group - 1):
            step1(i, j, bc).wait_send()
            step3(i, j, bc).wait_send()
        for j in range(depth - 1):
            step2(i, j, zc).wait_send()
    for s in range(SLOTS):
        adjoint_copy(s).wait_send()
    grad_copy.wait()
    wg_copy.wait()


def local(dom, chan, group, *arrays):
    features, _, weights, tile_values, tile_cols, send_list = arrays
    c, n = features.shape
    orders, _, all_c = weights.shape
    tiles, tile, _ = tile_values.shape
    halo = SLOTS * tile
    wide = n + halo
    depth, share = dom // group, c // group
    scale = float(dom * n) ** -0.5
    dma, vmem = pltpu.SemaphoreType.DMA, pltpu.VMEM
    anywhere = pl.BlockSpec(memory_space=pl.ANY)
    input_grad, weight_grad = pl.pallas_call(
        functools.partial(kernel, (dom, chan, group, scale)),
        out_shape=(
            jax.ShapeDtypeStruct((c, n), F32),
            jax.ShapeDtypeStruct((orders, c, all_c), F32),
        ),
        in_specs=[anywhere] * 6,
        out_specs=(anywhere, anywhere),
        scratch_shapes=[
            vmem((all_c, n), BF16),
            vmem((all_c, wide), BF16),
            vmem(weights.shape, BF16),
            vmem(tile_values.shape, F32),
            vmem((tile_cols.shape[-1] + 1, tile, tile), F32),
            pltpu.SMEM(tile_cols.shape, jnp.int32),
            vmem(send_list.shape, jnp.int32),
            vmem((n, halo), BF16),
            vmem((wide, wide), BF16),
            vmem((wide, wide), BF16),
            vmem((2, 2 * c, wide), F32),
            vmem((4 * c, n), BF16),
            vmem((2 * c, wide), F32),
            vmem((2, SLOTS, 4 * c, tile), BF16),
            vmem((2, SLOTS, 4 * c, tile), BF16),
            vmem((2 * c, n), BF16),
            vmem((SLOTS, tile, 2 * all_c), BF16),
            vmem((SLOTS, tile, 2 * all_c), BF16),
            vmem((n, all_c), F32),
            vmem((n, all_c), BF16),
            vmem((n, all_c), BF16),
            vmem((orders, c, all_c), F32),
            vmem((group, orders, share, all_c), F32),
            vmem((depth, orders, share, all_c), F32),
            vmem((orders, c, all_c), F32),
            dma((5,)),
            dma((n // tile,)),
            dma((2,)),
            dma((3, chan)),
            dma((3, chan)),
            dma((2, SLOTS)),
            dma((2, SLOTS)),
            dma((SLOTS,)),
            dma((SLOTS,)),
            *[dma((len(BATCHES), k)) for k in (group, depth, group)],
            *[dma((len(BATCHES), k)) for k in (group, depth, group)],
        ],
        compiler_params=pltpu.CompilerParams(
            collective_id=0, has_side_effects=True, vmem_limit_bytes=48 << 20
        ),
        name="clenshaw",
    )(*(pltpu.with_memory_space_constraint(x, pltpu.HBM) for x in arrays))
    return input_grad, jnp.swapaxes(weight_grad, 1, 2)


def solution(mesh):
    dom, chan = mesh.shape["dom"], mesh.shape["chan"]
    placed = (
        P("chan", "dom"),
        P("chan", "dom"),
        P(None, "chan", None),
        P("dom", None, None),
        P("dom", None, None),
        P("dom", None, None),
    )
    return jax.shard_map(
        functools.partial(local, dom, chan, 8),
        mesh=mesh,
        in_specs=placed,
        out_specs=(P("chan", "dom"), P(None, None, "chan")),
        check_vma=False,
    )
```

```python
import functools

import jax
import jax.numpy as jnp
from jax import lax
from jax.experimental import pallas as pl
from jax.experimental.pallas import tpu as pltpu
from jax.sharding import PartitionSpec as P

NEIGHBOUR_SHIFTS = (1, -1, 2, -2)
SLOTS = len(NEIGHBOUR_SHIFTS)
MESH = pl.DeviceIdType.MESH
LAST, AFTER = 8, 9
BATCHES = ((0, 3, 1, 4, 6), (3, 5, 3, 5, 7), (5, 7, 5, 6, LAST), (7, 9, 6, 7, AFTER))
ADJOINT = (2, 3, 2, 4)
F32, BF16 = jnp.float32, jnp.bfloat16


def dot(a, b):
    return jnp.dot(a, b, preferred_element_type=F32)


def dot_nt(a, b):
    return lax.dot_general(a, b, (((1,), (1,)), ((), ())), preferred_element_type=F32)


def split(x):
    hi = x.astype(BF16)
    return hi, (x - hi.astype(F32)).astype(BF16)


def kernel(
    dims,
    feat_hbm, cot_hbm, w_hbm, tiles_hbm, cols_hbm, send_hbm,
    grad_out, wg_out,
    feat, cotx, w, tiles, sums, cols, send, sel, e_hi, e_lo, state, parts, base,
    outbox, inbox, early, f_out, f_in, f_own, f_hi, f_lo, wg, wg_rows, wg_deep, wg_full,
    local_sem, tile_sem, out_sem, gather_send, gather_recv, halo_send, halo_recv, f_send, f_recv,
    s1, s2, s3, r1, r2, r3,
):
    dom, chan, group, scale = dims
    depth = dom // group
    me, xc = lax.axis_index("dom"), lax.axis_index("chan")
    zc, bc = me // group, lax.rem(me, group)
    top = w.shape[0] - 1
    c, n = feat_hbm.shape
    tile = tiles.shape[-1]
    halo = SLOTS * tile
    blocks = n // tile
    wide = n + halo
    per_row = tiles.shape[0] // blocks
    share = c // group
    all_c = feat.shape[0]

    def along_dom(index):
        return {"dom": index}

    halo_to = [along_dom(lax.rem(me + d + dom, dom)) for d in NEIGHBOUR_SHIFTS]
    chan_of = [lax.rem(xc + j, chan) for j in range(1, chan)]
    row_of = [lax.rem(bc + j, group) for j in range(1, group)]
    deep_of = [lax.rem(zc + j, depth) for j in range(1, depth)]
    row_to = [along_dom(zc * group + b) for b in row_of]
    deep_to = [along_dom(z * group + bc) for z in deep_of]

    def remote(src, dst, ssem, rsem, to):
        return pltpu.make_async_remote_copy(src, dst, ssem, rsem, device_id=to, device_id_type=MESH)

    my_rows = pl.ds(pl.multiple_of(xc * c, c), c)
    own_cot = cotx.at[my_rows, pl.ds(0, n)]
    own_feat = feat.at[my_rows, :]
    in_copies = [
        pltpu.make_async_copy(send_hbm, send, local_sem.at[0]),
        pltpu.make_async_copy(cot_hbm, own_cot, local_sem.at[1]),
        pltpu.make_async_copy(cols_hbm, cols, local_sem.at[2]),
        pltpu.make_async_copy(w_hbm, w, local_sem.at[3]),
        pltpu.make_async_copy(feat_hbm, own_feat, local_sem.at[4]),
    ]
    for copy in in_copies:
        copy.start()

    def tile_copy(r):
        rows = pl.ds(r * per_row, per_row)
        return pltpu.make_async_copy(tiles_hbm.at[rows], tiles.at[rows], tile_sem.at[r])

    for r in range(blocks):
        tile_copy(r).start()

    barrier = pltpu.get_barrier_semaphore()
    greeted = halo_to + [{"chan": x} for x in chan_of] + row_to + deep_to
    for peer in greeted:
        pl.semaphore_signal(barrier, inc=1, device_id=peer, device_id_type=MESH)

    in_copies[0].wait()
    node = lax.broadcasted_iota(jnp.int32, (n, tile), 0)
    for s in range(SLOTS):
        picked = send[0, s : s + 1, :]
        sel[:, s * tile : (s + 1) * tile] = jnp.where(node == picked, 1.0, 0.0).astype(BF16)
    in_copies[1].wait()
    first = cotx[my_rows, 0:n]
    first_sel = dot(first, sel[...])
    state[0, 0:c, 0:n] = first.astype(F32)
    state[0, 0:c, n:wide] = first_sel
    cotx[my_rows, n:wide] = first_sel.astype(BF16)
    state[0, c:, :] = jnp.zeros((c, wide), F32)
    state[1] = jnp.zeros((2 * c, wide), F32)
    parts[...] = jnp.zeros(parts.shape, BF16)
    parts[0:c] = first
    for s in range(SLOTS):
        outbox[0, s] = jnp.zeros(outbox.shape[2:], BF16)
        outbox[0, s, 0:c] = first_sel[:, s * tile : (s + 1) * tile].astype(BF16)

    def halo_copy(parity, s):
        return remote(
            outbox.at[parity, s], inbox.at[parity, s], halo_send.at[parity, s], halo_recv.at[parity, s], halo_to[s]
        )

    def gathered(which, x):
        rows = pl.ds(pl.multiple_of(x * c, c), c)
        return (cotx.at[rows, pl.ds(n, halo)], cotx.at[rows, pl.ds(0, n)], feat.at[rows, :])[which]

    def gather_copy(which, j):
        block = gathered(which, xc)
        return remote(block, block, gather_send.at[which, j], gather_recv.at[which, xc], {"chan": chan_of[j]})

    def gather_wait(which):
        for x in chan_of:
            block = gathered(which, x)
            remote(block, block, gather_send.at[which, 0], gather_recv.at[which, x], {"chan": x}).wait_recv()

    in_copies[2].wait()

    sums[per_row] = jnp.zeros((tile, tile), F32)

    def assemble(r, carry):
        tile_copy(r).wait()
        columns = pl.ds(pl.multiple_of(r * tile, tile), tile)
        block_of = [cols[0, r, j] for j in range(per_row)]
        for j in range(per_row):
            before = per_row
            for i in range(j):
                before = jnp.where(block_of[i] == block_of[j], i, before)
            mine = tiles[r * per_row + j]
            sums[j] = mine if j == 0 else mine + sums[before]
        for cb in range(blocks + SLOTS):
            last = per_row
            for j in range(per_row):
                last = jnp.where(block_of[j] == cb, j, last)
            hi, lo = split(sums[last])
            e_hi[cb * tile : (cb + 1) * tile, columns] = hi
            e_lo[cb * tile : (cb + 1) * tile, columns] = lo
        return carry

    lax.fori_loop(0, blocks, assemble, 0)

    pl.semaphore_wait(barrier, len(greeted))
    for s in range(SLOTS):
        halo_copy(0, s).start()
    for which in range(2):
        for j in range(chan - 1):
            gather_copy(which, j).start()

    for e in (e_hi, e_lo):
        for i in range(SLOTS // 2):
            at = slice(2 * i * tile, 2 * (i + 1) * tile)
            e[:, n + 2 * i * tile : n + 2 * (i + 1) * tile] = dot(e[:, 0:n], sel[:, at]).astype(BF16)

    chunk = halo

    def prepare(order, fac_u, fac_b, older):
        for i in range(wide // chunk):
            at = slice(i * chunk, (i + 1) * chunk)
            full = dot(parts[...], e_hi[0:n, at])
            part = full[0 : 2 * c] + full[2 * c :] + dot(parts[0 : 2 * c], e_lo[0:n, at])
            base[0:c, at] = fac_u * part[0:c] - state[older, 0:c, at]
            base[c:, at] = fac_b * part[c:] - state[older, c:, at]
            if order is not None:
                base[c:, at] += dot(w[order], cotx[:, at])

    def arrived(lhs, at):
        full = dot(lhs, e_hi[n:wide, at])
        return full[0 : 2 * c] + full[2 * c :] + dot(lhs[0 : 2 * c], e_lo[n:wide, at])

    def halo_in(parity):
        for s in range(SLOTS):
            halo_copy(parity, s).wait_recv()
        return jnp.concatenate([inbox[parity, s] for s in range(SLOTS)], axis=1)

    def row_part(b):
        return pl.ds(pl.multiple_of(b * share, share), share)

    def orders_of(i):
        low, high = BATCHES[i][:2]
        return pl.ds(low, high - low)

    def step1(i, j, sem_of):
        k = orders_of(i)
        return remote(wg.at[k, row_part(row_of[j])], wg_rows.at[sem_of, k], s1.at[i, j], r1.at[i, sem_of], row_to[j])

    def step2(i, j, sem_of):
        part = wg_deep.at[sem_of, orders_of(i)]
        return remote(part, part, s2.at[i, j], r2.at[i, sem_of], deep_to[j])

    def step3(i, j, sem_of):
        part = wg_full.at[orders_of(i), row_part(sem_of)]
        return remote(part, part, s3.at[i, j], r3.at[i, sem_of], row_to[j])

    def send_rows(i):
        k = orders_of(i)
        for j in range(group - 1):
            step1(i, j, bc).start()
        wg_rows[bc, k] = wg[k, row_part(bc), :]

    def send_deep(i):
        k = orders_of(i)
        for j in range(group - 1):
            step1(i, j, row_of[j]).wait_recv()
        total = wg_rows[0, k]
        for j in range(1, group):
            total += wg_rows[j, k]
        wg_deep[zc, k] = total
        for j in range(depth - 1):
            step2(i, j, zc).start()

    def send_back(i):
        k = orders_of(i)
        for j in range(depth - 1):
            step2(i, j, deep_of[j]).wait_recv()
        total = wg_deep[0, k]
        for j in range(1, depth):
            total += wg_deep[j, k]
        wg_full[k, row_part(bc), :] = total * scale
        for j in range(group - 1):
            step3(i, j, bc).start()

    def at_round(r, column, step, among=range(len(BATCHES))):
        for i in among:
            if BATCHES[i][column] < top:
                pl.when(r == BATCHES[i][column])(functools.partial(step, i))

    def adjoint_copy(s):
        to = along_dom(lax.rem(me - NEIGHBOUR_SHIFTS[s] + dom, dom))
        return remote(f_out.at[s], f_in.at[s], f_send.at[s], f_recv.at[s], to)

    def adjoint_rows(rows):
        return dot_nt(e_hi[rows, 0:n], feat[...]) + dot_nt(e_lo[rows, 0:n], feat[...])

    def adjoint_out():
        hi, lo = split(adjoint_rows(slice(n, wide)))
        for s in range(SLOTS):
            rows = slice(s * tile, (s + 1) * tile)
            f_out[s, :, 0:all_c] = hi[rows]
            f_out[s, :, all_c:] = lo[rows]

    def adjoint_send():
        for s in range(SLOTS):
            adjoint_copy(s).start()

    def adjoint_own():
        f_own[...] = adjoint_rows(slice(0, n))

    def adjoint_in():
        for s in range(SLOTS):
            adjoint_copy(s).wait_recv()
        both = dot(sel[...], f_in[...].reshape(halo, 2 * all_c))
        hi, lo = split(f_own[...] + both[:, 0:all_c] + both[:, all_c:])
        f_hi[...] = hi
        f_lo[...] = lo

    prepare(None, 1.0, 2.0, 1)
    in_copies[3].wait()
    gather_wait(0)
    base[c:, n:wide] += dot(w[top], cotx[:, n:wide])

    def round_(r, carry):
        parity = lax.rem(r, 2)
        other = 1 - parity
        fac_u = jnp.where(r == 0, 1.0, 2.0).astype(F32)
        lhs = halo_in(parity)
        at = slice(n, wide)
        got = arrived(lhs, at)
        next_u = base[0:c, at] + fac_u * got[0:c]
        next_b = base[c:, at] + 2.0 * got[c:]
        state[other, 0:c, at] = next_u
        state[other, c:, at] = next_b
        u_hi, u_lo = split(next_u)
        b_hi, b_lo = split(next_b)

        @pl.when(r > 0)
        def _():
            for s in range(SLOTS):
                halo_copy(other, s).wait_send()

        for s in range(SLOTS):
            cut = slice(s * tile, (s + 1) * tile)
            for i, piece in enumerate((u_hi, b_hi, u_lo, b_lo)):
                outbox[other, s, i * c : (i + 1) * c] = piece[:, cut]
        for s in range(SLOTS):
            halo_copy(other, s).start()

        @pl.when(r == 0)
        def _():
            gather_wait(1)
            in_copies[4].wait()
            for j in range(chan - 1):
                gather_copy(2, j).start()
            base[c:, 0:n] += dot(w[top], cotx[:, 0:n])

        pl.when(r == ADJOINT[1])(adjoint_send)
        at_round(r, 3, send_deep)
        at_round(r, 4, send_back)

        for i in range(n // chunk):
            at = slice(i * chunk, (i + 1) * chunk)
            got = arrived(lhs, at)
            next_u = base[0:c, at] + fac_u * got[0:c]
            next_b = base[c:, at] + 2.0 * got[c:]
            state[other, 0:c, at] = next_u
            state[other, c:, at] = next_b
            for j, piece in enumerate((*split(next_u), *split(next_b))):
                row = (0, 2, 1, 3)[j] * c
                parts[row : row + c, at] = piece

        def now():
            return jnp.concatenate([parts[0:c], parts[2 * c : 3 * c]], axis=0)

        def weigh(k, field):
            both = dot_nt(field, feat[...])
            wg[k] = both[0:c] + both[c:]

        @pl.when(r == 0)
        def _():
            early[...] = now()

        @pl.when(jnp.logical_and(r > 1, r < top - 1))
        def _():
            weigh(r + 1, now())

        @pl.when(r == top - 2)
        def _():
            both = dot(now(), f_hi[...])
            twice = both[0:c] + both[c:] + dot(parts[0:c], f_lo[...])
            wg[top] = 2.0 * twice - wg[top - 2]

        at_round(r, 2, send_rows, range(1, len(BATCHES)))
        prepare(top - 1 - r, 2.0, jnp.where(r == top - 1, 1.0, 2.0).astype(F32), parity)

        @pl.when(r == 1)
        def _():
            gather_wait(2)
            wg[0] = dot_nt(cotx[my_rows, 0:n], feat[...])
            weigh(1, early[...])
            weigh(2, now())
            send_rows(0)

        for at, step in zip(ADJOINT[::2] + ADJOINT[3:], (adjoint_out, adjoint_own, adjoint_in)):
            pl.when(r == at)(step)
        return carry

    lax.fori_loop(0, top, round_, 0)

    def send_back_at(place):
        for i in range(len(BATCHES)):
            if BATCHES[i][4] == place:
                send_back(i)

    send_back_at(LAST)
    last = top % 2
    lhs = halo_in(last)
    for i in range(n // chunk):
        at = slice(i * chunk, (i + 1) * chunk)
        base[c:, at] = base[c:, at] + arrived(lhs, at)[c:]
    grad_copy = pltpu.make_async_copy(base.at[pl.ds(c, c), pl.ds(0, n)], grad_out, out_sem.at[0])
    grad_copy.start()
    send_back_at(AFTER)
    for i in range(len(BATCHES)):
        for j in range(group - 1):
            step3(i, j, row_of[j]).wait_recv()
    wg_copy = pltpu.make_async_copy(wg_full, wg_out, out_sem.at[1])
    wg_copy.start()

    for which in range(3):
        for j in range(chan - 1):
            gather_copy(which, j).wait_send()
    for parity in range(2):
        for s in range(SLOTS):
            halo_copy(parity, s).wait_send()
    for i in range(len(BATCHES)):
        for j in range(group - 1):
            step1(i, j, bc).wait_send()
            step3(i, j, bc).wait_send()
        for j in range(depth - 1):
            step2(i, j, zc).wait_send()
    for s in range(SLOTS):
        adjoint_copy(s).wait_send()
    grad_copy.wait()
    wg_copy.wait()


def local(dom, chan, group, *arrays):
    features, _, weights, tile_values, tile_cols, send_list = arrays
    c, n = features.shape
    orders, _, all_c = weights.shape
    tiles, tile, _ = tile_values.shape
    halo = SLOTS * tile
    wide = n + halo
    depth, share = dom // group, c // group
    scale = float(dom * n) ** -0.5
    dma, vmem = pltpu.SemaphoreType.DMA, pltpu.VMEM
    anywhere = pl.BlockSpec(memory_space=pl.ANY)
    input_grad, weight_grad = pl.pallas_call(
        functools.partial(kernel, (dom, chan, group, scale)),
        out_shape=(
            jax.ShapeDtypeStruct((c, n), F32),
            jax.ShapeDtypeStruct((orders, c, all_c), F32),
        ),
        in_specs=[anywhere] * 6,
        out_specs=(anywhere, anywhere),
        scratch_shapes=[
            vmem((all_c, n), BF16),
            vmem((all_c, wide), BF16),
            vmem(weights.shape, BF16),
            vmem(tile_values.shape, F32),
            vmem((tile_cols.shape[-1] + 1, tile, tile), F32),
            pltpu.SMEM(tile_cols.shape, jnp.int32),
            vmem(send_list.shape, jnp.int32),
            vmem((n, halo), BF16),
            vmem((wide, wide), BF16),
            vmem((wide, wide), BF16),
            vmem((2, 2 * c, wide), F32),
            vmem((4 * c, n), BF16),
            vmem((2 * c, wide), F32),
            vmem((2, SLOTS, 4 * c, tile), BF16),
            vmem((2, SLOTS, 4 * c, tile), BF16),
            vmem((2 * c, n), BF16),
            vmem((SLOTS, tile, 2 * all_c), BF16),
            vmem((SLOTS, tile, 2 * all_c), BF16),
            vmem((n, all_c), F32),
            vmem((n, all_c), BF16),
            vmem((n, all_c), BF16),
            vmem((orders, c, all_c), F32),
            vmem((group, orders, share, all_c), F32),
            vmem((depth, orders, share, all_c), F32),
            vmem((orders, c, all_c), F32),
            dma((5,)),
            dma((n // tile,)),
            dma((2,)),
            dma((3, chan)),
            dma((3, chan)),
            dma((2, SLOTS)),
            dma((2, SLOTS)),
            dma((SLOTS,)),
            dma((SLOTS,)),
            *[dma((len(BATCHES), k)) for k in (group, depth, group)],
            *[dma((len(BATCHES), k)) for k in (group, depth, group)],
        ],
        compiler_params=pltpu.CompilerParams(
            collective_id=0, has_side_effects=True, vmem_limit_bytes=48 << 20
        ),
        name="clenshaw",
    )(*(pltpu.with_memory_space_constraint(x, pltpu.HBM) for x in arrays))
    return input_grad, jnp.swapaxes(weight_grad, 1, 2)


def solution(mesh):
    dom, chan = mesh.shape["dom"], mesh.shape["chan"]
    placed = (
        P("chan", "dom"),
        P("chan", "dom"),
        P(None, "chan", None),
        P("dom", None, None),
        P("dom", None, None),
        P("dom", None, None),
    )
    return jax.shard_map(
        functools.partial(local, dom, chan, 8),
        mesh=mesh,
        in_specs=placed,
        out_specs=(P("chan", "dom"), P(None, None, "chan")),
        check_vma=False,
    )
```

```python
import functools

import jax
import jax.numpy as jnp
from jax import lax
from jax.experimental import pallas as pl
from jax.experimental.pallas import tpu as pltpu
from jax.sharding import PartitionSpec as P

NEIGHBOUR_SHIFTS = (1, -1, 2, -2)
SLOTS = len(NEIGHBOUR_SHIFTS)
MESH = pl.DeviceIdType.MESH
LAST, AFTER = 8, 9
BATCHES = ((0, 3, 1, 4, 6), (3, 5, 3, 5, 7), (5, 7, 5, 6, LAST), (7, 9, 6, 7, AFTER))
ADJOINT = (2, 3, 2, 4)
F32, BF16 = jnp.float32, jnp.bfloat16


def dot(a, b):
    return jnp.dot(a, b, preferred_element_type=F32)


def dot_nt(a, b):
    return lax.dot_general(a, b, (((1,), (1,)), ((), ())), preferred_element_type=F32)


def split(x):
    hi = x.astype(BF16)
    return hi, (x - hi.astype(F32)).astype(BF16)


def kernel(
    dims,
    feat_hbm, cot_hbm, w_hbm, tiles_hbm, cols_hbm, send_hbm,
    grad_out, wg_out,
    feat, cotx, w, tiles, sums, cols, send, sel, e_hi, e_lo, state, parts, base,
    outbox, inbox, early, f_out, f_in, f_own, f_hi, f_lo, wg, wg_rows, wg_deep, wg_full,
    local_sem, tile_sem, out_sem, gather_send, gather_recv, halo_send, halo_recv, f_send, f_recv,
    s1, s2, s3, r1, r2, r3,
):
    dom, chan, group, scale = dims
    depth = dom // group
    me, xc = lax.axis_index("dom"), lax.axis_index("chan")
    zc, bc = me // group, lax.rem(me, group)
    top = w.shape[0] - 1
    c, n = feat_hbm.shape
    tile = tiles.shape[-1]
    halo = SLOTS * tile
    blocks = n // tile
    wide = n + halo
    per_row = tiles.shape[0] // blocks
    share = c // group
    all_c = feat.shape[0]

    def along_dom(index):
        return {"dom": index}

    halo_to = [along_dom(lax.rem(me + d + dom, dom)) for d in NEIGHBOUR_SHIFTS]
    chan_of = [lax.rem(xc + j, chan) for j in range(1, chan)]
    row_of = [lax.rem(bc + j, group) for j in range(1, group)]
    deep_of = [lax.rem(zc + j, depth) for j in range(1, depth)]
    row_to = [along_dom(zc * group + b) for b in row_of]
    deep_to = [along_dom(z * group + bc) for z in deep_of]

    def remote(src, dst, ssem, rsem, to):
        return pltpu.make_async_remote_copy(src, dst, ssem, rsem, device_id=to, device_id_type=MESH)

    my_rows = pl.ds(pl.multiple_of(xc * c, c), c)
    own_cot = cotx.at[my_rows, pl.ds(0, n)]
    own_feat = feat.at[my_rows, :]
    in_copies = [
        pltpu.make_async_copy(send_hbm, send, local_sem.at[0]),
        pltpu.make_async_copy(cot_hbm, own_cot, local_sem.at[1]),
        pltpu.make_async_copy(cols_hbm, cols, local_sem.at[2]),
        pltpu.make_async_copy(w_hbm, w, local_sem.at[3]),
        pltpu.make_async_copy(feat_hbm, own_feat, local_sem.at[4]),
    ]
    for copy in in_copies:
        copy.start()

    def tile_copy(r):
        rows = pl.ds(r * per_row, per_row)
        return pltpu.make_async_copy(tiles_hbm.at[rows], tiles.at[rows], tile_sem.at[r])

    for r in range(blocks):
        tile_copy(r).start()

    barrier = pltpu.get_barrier_semaphore()
    greeted = halo_to + [{"chan": x} for x in chan_of] + row_to + deep_to
    for peer in greeted:
        pl.semaphore_signal(barrier, inc=1, device_id=peer, device_id_type=MESH)

    in_copies[0].wait()
    node = lax.broadcasted_iota(jnp.int32, (n, tile), 0)
    for s in range(SLOTS):
        picked = send[0, s : s + 1, :]
        sel[:, s * tile : (s + 1) * tile] = jnp.where(node == picked, 1.0, 0.0).astype(BF16)
    in_copies[1].wait()
    first = cotx[my_rows, 0:n]
    first_sel = dot(first, sel[...])
    state[0, 0:c, 0:n] = first.astype(F32)
    state[0, 0:c, n:wide] = first_sel
    cotx[my_rows, n:wide] = first_sel.astype(BF16)
    state[0, c:, :] = jnp.zeros((c, wide), F32)
    state[1] = jnp.zeros((2 * c, wide), F32)
    parts[...] = jnp.zeros(parts.shape, BF16)
    parts[0:c] = first
    for s in range(SLOTS):
        outbox[0, s] = jnp.zeros(outbox.shape[2:], BF16)
        outbox[0, s, 0:c] = first_sel[:, s * tile : (s + 1) * tile].astype(BF16)

    def halo_copy(parity, s):
        return remote(
            outbox.at[parity, s], inbox.at[parity, s], halo_send.at[parity, s], halo_recv.at[parity, s], halo_to[s]
        )

    def gathered(which, x):
        rows = pl.ds(pl.multiple_of(x * c, c), c)
        return (cotx.at[rows, pl.ds(n, halo)], cotx.at[rows, pl.ds(0, n)], feat.at[rows, :])[which]

    def gather_copy(which, j):
        block = gathered(which, xc)
        return remote(block, block, gather_send.at[which, j], gather_recv.at[which, xc], {"chan": chan_of[j]})

    def gather_wait(which):
        for x in chan_of:
            block = gathered(which, x)
            remote(block, block, gather_send.at[which, 0], gather_recv.at[which, x], {"chan": x}).wait_recv()

    in_copies[2].wait()

    sums[per_row] = jnp.zeros((tile, tile), F32)

    def assemble(r, carry):
        tile_copy(r).wait()
        columns = pl.ds(pl.multiple_of(r * tile, tile), tile)
        block_of = [cols[0, r, j] for j in range(per_row)]
        for j in range(per_row):
            before = per_row
            for i in range(j):
                before = jnp.where(block_of[i] == block_of[j], i, before)
            mine = tiles[r * per_row + j]
            sums[j] = mine if j == 0 else mine + sums[before]
        for cb in range(blocks + SLOTS):
            last = per_row
            for j in range(per_row):
                last = jnp.where(block_of[j] == cb, j, last)
            hi, lo = split(sums[last])
            e_hi[cb * tile : (cb + 1) * tile, columns] = hi
            e_lo[cb * tile : (cb + 1) * tile, columns] = lo
        return carry

    lax.fori_loop(0, blocks, assemble, 0)

    pl.semaphore_wait(barrier, len(greeted))
    for s in range(SLOTS):
        halo_copy(0, s).start()
    for which in range(2):
        for j in range(chan - 1):
            gather_copy(which, j).start()

    for e in (e_hi, e_lo):
        for i in range(SLOTS // 2):
            at = slice(2 * i * tile, 2 * (i + 1) * tile)
            e[:, n + 2 * i * tile : n + 2 * (i + 1) * tile] = dot(e[:, 0:n], sel[:, at]).astype(BF16)

    chunk = halo

    def prepare(order, fac_u, fac_b, older):
        for i in range(wide // chunk):
            at = slice(i * chunk, (i + 1) * chunk)
            full = dot(parts[...], e_hi[0:n, at])
            part = full[0 : 2 * c] + full[2 * c :] + dot(parts[0 : 2 * c], e_lo[0:n, at])
            base[0:c, at] = fac_u * part[0:c] - state[older, 0:c, at]
            base[c:, at] = fac_b * part[c:] - state[older, c:, at]
            if order is not None:
                base[c:, at] += dot(w[order], cotx[:, at])

    def arrived(lhs, at):
        full = dot(lhs, e_hi[n:wide, at])
        return full[0 : 2 * c] + full[2 * c :] + dot(lhs[0 : 2 * c], e_lo[n:wide, at])

    def halo_in(parity):
        for s in range(SLOTS):
            halo_copy(parity, s).wait_recv()
        return jnp.concatenate([inbox[parity, s] for s in range(SLOTS)], axis=1)

    def row_part(b):
        return pl.ds(pl.multiple_of(b * share, share), share)

    def orders_of(i):
        low, high = BATCHES[i][:2]
        return pl.ds(low, high - low)

    def step1(i, j, sem_of):
        k = orders_of(i)
        return remote(wg.at[k, row_part(row_of[j])], wg_rows.at[sem_of, k], s1.at[i, j], r1.at[i, sem_of], row_to[j])

    def step2(i, j, sem_of):
        part = wg_deep.at[sem_of, orders_of(i)]
        return remote(part, part, s2.at[i, j], r2.at[i, sem_of], deep_to[j])

    def step3(i, j, sem_of):
        part = wg_full.at[orders_of(i), row_part(sem_of)]
        return remote(part, part, s3.at[i, j], r3.at[i, sem_of], row_to[j])

    def send_rows(i):
        k = orders_of(i)
        for j in range(group - 1):
            step1(i, j, bc).start()
        wg_rows[bc, k] = wg[k, row_part(bc), :]

    def send_deep(i):
        k = orders_of(i)
        for j in range(group - 1):
            step1(i, j, row_of[j]).wait_recv()
        total = wg_rows[0, k]
        for j in range(1, group):
            total += wg_rows[j, k]
        wg_deep[zc, k] = total
        for j in range(depth - 1):
            step2(i, j, zc).start()

    def send_back(i):
        k = orders_of(i)
        for j in range(depth - 1):
            step2(i, j, deep_of[j]).wait_recv()
        total = wg_deep[0, k]
        for j in range(1, depth):
            total += wg_deep[j, k]
        wg_full[k, row_part(bc), :] = total * scale
        for j in range(group - 1):
            step3(i, j, bc).start()

    def at_round(r, column, step, among=range(len(BATCHES))):
        for i in among:
            if BATCHES[i][column] < top:
                pl.when(r == BATCHES[i][column])(functools.partial(step, i))

    def adjoint_copy(s):
        to = along_dom(lax.rem(me - NEIGHBOUR_SHIFTS[s] + dom, dom))
        return remote(f_out.at[s], f_in.at[s], f_send.at[s], f_recv.at[s], to)

    def adjoint_rows(rows):
        return dot_nt(e_hi[rows, 0:n], feat[...]) + dot_nt(e_lo[rows, 0:n], feat[...])

    def adjoint_out():
        hi, lo = split(adjoint_rows(slice(n, wide)))
        for s in range(SLOTS):
            rows = slice(s * tile, (s + 1) * tile)
            f_out[s, :, 0:all_c] = hi[rows]
            f_out[s, :, all_c:] = lo[rows]

    def adjoint_send():
        for s in range(SLOTS):
            adjoint_copy(s).start()

    def adjoint_own():
        f_own[...] = adjoint_rows(slice(0, n))

    def adjoint_in():
        for s in range(SLOTS):
            adjoint_copy(s).wait_recv()
        both = dot(sel[...], f_in[...].reshape(halo, 2 * all_c))
        hi, lo = split(f_own[...] + both[:, 0:all_c] + both[:, all_c:])
        f_hi[...] = hi
        f_lo[...] = lo

    prepare(None, 1.0, 2.0, 1)
    in_copies[3].wait()
    gather_wait(0)
    base[c:, n:wide] += dot(w[top], cotx[:, n:wide])

    def round_(r, carry):
        parity = lax.rem(r, 2)
        other = 1 - parity
        fac_u = jnp.where(r == 0, 1.0, 2.0).astype(F32)
        lhs = halo_in(parity)
        at = slice(n, wide)
        got = arrived(lhs, at)
        next_u = base[0:c, at] + fac_u * got[0:c]
        next_b = base[c:, at] + 2.0 * got[c:]
        state[other, 0:c, at] = next_u
        state[other, c:, at] = next_b
        u_hi, u_lo = split(next_u)
        b_hi, b_lo = split(next_b)

        @pl.when(r > 0)
        def _():
            for s in range(SLOTS):
                halo_copy(other, s).wait_send()

        for s in range(SLOTS):
            cut = slice(s * tile, (s + 1) * tile)
            for i, piece in enumerate((u_hi, b_hi, u_lo, b_lo)):
                outbox[other, s, i * c : (i + 1) * c] = piece[:, cut]
        for s in range(SLOTS):
            halo_copy(other, s).start()

        @pl.when(r == 0)
        def _():
            gather_wait(1)
            in_copies[4].wait()
            for j in range(chan - 1):
                gather_copy(2, j).start()
            base[c:, 0:n] += dot(w[top], cotx[:, 0:n])

        pl.when(r == ADJOINT[1])(adjoint_send)
        busy = top - 2
        for column, step in ((3, send_deep), (4, send_back)):
            at_round(r, column, step, [i for i in range(len(BATCHES)) if BATCHES[i][column] != busy])

        for i in range(n // chunk):
            at = slice(i * chunk, (i + 1) * chunk)
            got = arrived(lhs, at)
            next_u = base[0:c, at] + fac_u * got[0:c]
            next_b = base[c:, at] + 2.0 * got[c:]
            state[other, 0:c, at] = next_u
            state[other, c:, at] = next_b
            for j, piece in enumerate((*split(next_u), *split(next_b))):
                row = (0, 2, 1, 3)[j] * c
                parts[row : row + c, at] = piece

        def now():
            return jnp.concatenate([parts[0:c], parts[2 * c : 3 * c]], axis=0)

        def weigh(k, field):
            both = dot_nt(field, feat[...])
            wg[k] = both[0:c] + both[c:]

        @pl.when(r == 0)
        def _():
            early[...] = now()

        @pl.when(jnp.logical_and(r > 1, r < top - 1))
        def _():
            weigh(r + 1, now())

        @pl.when(r == top - 2)
        def _():
            both = dot(now(), f_hi[...])
            twice = both[0:c] + both[c:] + dot(parts[0:c], f_lo[...])
            wg[top] = 2.0 * twice - wg[top - 2]

        at_round(r, 2, send_rows, range(1, len(BATCHES)))
        for column, step in ((3, send_deep), (4, send_back)):
            at_round(r, column, step, [i for i in range(len(BATCHES)) if BATCHES[i][column] == busy])
        prepare(top - 1 - r, 2.0, jnp.where(r == top - 1, 1.0, 2.0).astype(F32), parity)

        @pl.when(r == 1)
        def _():
            gather_wait(2)
            wg[0] = dot_nt(cotx[my_rows, 0:n], feat[...])
            weigh(1, early[...])
            weigh(2, now())
            send_rows(0)

        for at, step in zip(ADJOINT[::2] + ADJOINT[3:], (adjoint_out, adjoint_own, adjoint_in)):
            pl.when(r == at)(step)
        return carry

    lax.fori_loop(0, top, round_, 0)

    def send_back_at(place):
        for i in range(len(BATCHES)):
            if BATCHES[i][4] == place:
                send_back(i)

    send_back_at(LAST)
    last = top % 2
    lhs = halo_in(last)
    for i in range(n // chunk):
        at = slice(i * chunk, (i + 1) * chunk)
        base[c:, at] = base[c:, at] + arrived(lhs, at)[c:]
    grad_copy = pltpu.make_async_copy(base.at[pl.ds(c, c), pl.ds(0, n)], grad_out, out_sem.at[0])
    grad_copy.start()
    send_back_at(AFTER)
    for i in range(len(BATCHES)):
        for j in range(group - 1):
            step3(i, j, row_of[j]).wait_recv()
    wg_copy = pltpu.make_async_copy(wg_full, wg_out, out_sem.at[1])
    wg_copy.start()

    for which in range(3):
        for j in range(chan - 1):
            gather_copy(which, j).wait_send()
    for parity in range(2):
        for s in range(SLOTS):
            halo_copy(parity, s).wait_send()
    for i in range(len(BATCHES)):
        for j in range(group - 1):
            step1(i, j, bc).wait_send()
            step3(i, j, bc).wait_send()
        for j in range(depth - 1):
            step2(i, j, zc).wait_send()
    for s in range(SLOTS):
        adjoint_copy(s).wait_send()
    grad_copy.wait()
    wg_copy.wait()


def local(dom, chan, group, *arrays):
    features, _, weights, tile_values, tile_cols, send_list = arrays
    c, n = features.shape
    orders, _, all_c = weights.shape
    tiles, tile, _ = tile_values.shape
    halo = SLOTS * tile
    wide = n + halo
    depth, share = dom // group, c // group
    scale = float(dom * n) ** -0.5
    dma, vmem = pltpu.SemaphoreType.DMA, pltpu.VMEM
    anywhere = pl.BlockSpec(memory_space=pl.ANY)
    input_grad, weight_grad = pl.pallas_call(
        functools.partial(kernel, (dom, chan, group, scale)),
        out_shape=(
            jax.ShapeDtypeStruct((c, n), F32),
            jax.ShapeDtypeStruct((orders, c, all_c), F32),
        ),
        in_specs=[anywhere] * 6,
        out_specs=(anywhere, anywhere),
        scratch_shapes=[
            vmem((all_c, n), BF16),
            vmem((all_c, wide), BF16),
            vmem(weights.shape, BF16),
            vmem(tile_values.shape, F32),
            vmem((tile_cols.shape[-1] + 1, tile, tile), F32),
            pltpu.SMEM(tile_cols.shape, jnp.int32),
            vmem(send_list.shape, jnp.int32),
            vmem((n, halo), BF16),
            vmem((wide, wide), BF16),
            vmem((wide, wide), BF16),
            vmem((2, 2 * c, wide), F32),
            vmem((4 * c, n), BF16),
            vmem((2 * c, wide), F32),
            vmem((2, SLOTS, 4 * c, tile), BF16),
            vmem((2, SLOTS, 4 * c, tile), BF16),
            vmem((2 * c, n), BF16),
            vmem((SLOTS, tile, 2 * all_c), BF16),
            vmem((SLOTS, tile, 2 * all_c), BF16),
            vmem((n, all_c), F32),
            vmem((n, all_c), BF16),
            vmem((n, all_c), BF16),
            vmem((orders, c, all_c), F32),
            vmem((group, orders, share, all_c), F32),
            vmem((depth, orders, share, all_c), F32),
            vmem((orders, c, all_c), F32),
            dma((5,)),
            dma((n // tile,)),
            dma((2,)),
            dma((3, chan)),
            dma((3, chan)),
            dma((2, SLOTS)),
            dma((2, SLOTS)),
            dma((SLOTS,)),
            dma((SLOTS,)),
            *[dma((len(BATCHES), k)) for k in (group, depth, group)],
            *[dma((len(BATCHES), k)) for k in (group, depth, group)],
        ],
        compiler_params=pltpu.CompilerParams(
            collective_id=0, has_side_effects=True, vmem_limit_bytes=48 << 20
        ),
        name="clenshaw",
    )(*(pltpu.with_memory_space_constraint(x, pltpu.HBM) for x in arrays))
    return input_grad, jnp.swapaxes(weight_grad, 1, 2)


def solution(mesh):
    dom, chan = mesh.shape["dom"], mesh.shape["chan"]
    placed = (
        P("chan", "dom"),
        P("chan", "dom"),
        P(None, "chan", None),
        P("dom", None, None),
        P("dom", None, None),
        P("dom", None, None),
    )
    return jax.shard_map(
        functools.partial(local, dom, chan, 8),
        mesh=mesh,
        in_specs=placed,
        out_specs=(P("chan", "dom"), P(None, None, "chan")),
        check_vma=False,
    )
```
